32 devices in a mesh: grp: 1, row: 8 (over z, y), col: 2 (over x), ch: 2 (over core).
Axes of the slice: x: 2, y: 2, z: 4, core: 2. Of those that a mesh axis runs over, the one named last changes fastest.
Arguments:
- pair_input: float32 [96, 96, 128], P(('grp', 'row'), ('col', 'ch')), may hold values from -6 to 6
- saved_product: float32 [96, 96, 128], P(('grp', 'row'), ('col', 'ch')), may hold values from -6 to 6
- pair_grad: float32 [96, 96, 128], P(('grp', 'row'), ('col', 'ch')), may hold values from -6 to 6
- token_mask: int32 [96], P('grp'), may hold values 0 or 1
- w_one: float32 [128, 512], replicated, may hold values from -0.5 to 0.5
- w_two: float32 [128, 512], replicated, may hold values from -0.5 to 0.5
- w_three: float32 [512, 128], replicated, may hold values from -0.25 to 0.25
- w_left: float32 [128, 128], replicated, may hold values from -0.5 to 0.5
- w_left_gate: float32 [128, 128], replicated, may hold values from -0.5 to 0.5
- w_right: float32 [128, 128], replicated, may hold values from -0.5 to 0.5
- w_right_gate: float32 [128, 128], replicated, may hold values from -0.5 to 0.5
- w_out: float32 [128, 128], replicated, may hold values from -0.5 to 0.5
- w_out_gate: float32 [128, 128], replicated, may hold values from -0.5 to 0.5
Outputs:
- input_grad: float32 [96, 96, 128], P(('grp', 'row'), ('col', 'ch'))
The draws below stay inside these ranges and needn't reach their ends.
All inputs are finite; a program needn't handle non-finite values.
Results may differ from the reference program's by a relative error of at most 0.0038.
Values may be sent and summed in bfloat16 or wider, within the bound.
A program may use at most 128 MiB of HBM per device.

```python
import jax
import jax.numpy as jnp
from jax import lax

CH = 128
HID = 512
TOKENS = 96


def with_ends(values, stream_key, low, top_value):
    spot = [jax.random.randint(jax.random.fold_in(stream_key, axis), (), 0, length) for axis, length in enumerate(values.shape)]
    widest = values.shape.index(max(values.shape))
    neighbour = spot[:widest] + [(spot[widest] + 1) % values.shape[widest]] + spot[widest + 1:]
    return values.at[tuple(spot)].set(low).at[tuple(neighbour)].set(top_value)


def level_of(key, dims, pieces, smallest, largest):
    gain, own = 1.0, jax.random.fold_in(key, 6)
    for dim, parts in pieces:
        heights = jnp.exp(jax.random.uniform(jax.random.fold_in(own, dim), (parts,), jnp.float32, smallest / len(pieces), largest / len(pieces)))
        gain = gain * jnp.repeat(heights, dims[dim] // parts).reshape([-1 if axis == dim else 1 for axis in range(len(dims))])
    return gain


def scatter_about(stream_key, dims, width, bound, cuts=(), kind=jnp.bfloat16):
    values = jax.random.normal(stream_key, dims, jnp.float32) * width
    if len(cuts) > 0:
        values = level_of(stream_key, dims, cuts, -0.22, 0.18) * values
    return jnp.clip(values, min=-bound, max=bound).astype(kind)


def setup_inputs(seed: int = 0, part: int = 0) -> dict:
    keys = jax.random.split(jax.random.key(seed), 14)
    part_splits = jax.random.split(jax.random.fold_in(keys[13], part), 14)
    return {
        "pair_input": scatter_about(part_splits[0], (TOKENS, TOKENS, CH), 1.0, 6.0, ((0, 8), (1, 4)), jnp.float32),
        "saved_product": scatter_about(part_splits[1], (TOKENS, TOKENS, CH), 1.0, 6.0, ((0, 8), (1, 4)), jnp.float32),
        "pair_grad": scatter_about(part_splits[2], (TOKENS, TOKENS, CH), 1.0, 6.0, ((0, 8), (1, 4)), jnp.float32),
        "token_mask": with_ends((jax.random.randint(part_splits[3], (TOKENS,), 0, 8) < 7).astype(jnp.int32), jax.random.fold_in(part_splits[3], 1), 0, 1),
        "w_one": scatter_about(keys[4], (CH, HID), CH ** -0.5, 0.5, (), jnp.float32),
        "w_two": scatter_about(keys[5], (CH, HID), CH ** -0.5, 0.5, (), jnp.float32),
        "w_three": scatter_about(keys[6], (HID, CH), HID ** -0.5, 0.25, (), jnp.float32),
        "w_left": scatter_about(keys[7], (CH, CH), CH ** -0.5, 0.5, (), jnp.float32),
        "w_left_gate": scatter_about(keys[8], (CH, CH), CH ** -0.5, 0.5, (), jnp.float32),
        "w_right": scatter_about(keys[9], (CH, CH), CH ** -0.5, 0.5, (), jnp.float32),
        "w_right_gate": scatter_about(keys[10], (CH, CH), CH ** -0.5, 0.5, (), jnp.float32),
        "w_out": scatter_about(keys[11], (CH, CH), CH ** -0.5, 0.5, (), jnp.float32),
        "w_out_gate": scatter_about(keys[12], (CH, CH), CH ** -0.5, 0.5, (), jnp.float32),
    }


epsilon = 1e-05

def matmul(left, right):
    return jnp.dot(left, right, precision=lax.Precision.HIGHEST, preferred_element_type=jnp.float32)

def normalize(values):
    center = values - lax.optimization_barrier(jnp.mean(values, axis=-1, keepdims=True))
    inv_std = lax.rsqrt(lax.optimization_barrier(jnp.mean(center * center, axis=-1, keepdims=True)) + epsilon)
    return (center * inv_std, inv_std)

def norm_back(normed, inv_std, upstream):
    mean_up = lax.optimization_barrier(jnp.mean(upstream, axis=-1, keepdims=True))
    mean_proj = lax.optimization_barrier(jnp.mean(upstream * normed, axis=-1, keepdims=True))
    return (upstream - mean_up - normed * mean_proj) * inv_std

def local_front(pair_input, saved_product, pair_grad, pair_mask, w_one, w_two, w_three, w_left, w_left_gate, w_right, w_right_gate, w_out, w_out_gate):
    normed_in, inv_in = normalize(pair_input)
    hidden_one = matmul(normed_in, w_one)
    hidden_two = matmul(normed_in, w_two)
    updated = pair_input + matmul(jax.nn.silu(hidden_one) * hidden_two, w_three)
    normed_mid, inv_mid = normalize(updated)
    left_proj = matmul(normed_mid, w_left)
    left_gate = jax.nn.sigmoid(matmul(normed_mid, w_left_gate))
    right_proj = matmul(normed_mid, w_right)
    right_gate = jax.nn.sigmoid(matmul(normed_mid, w_right_gate))
    left_op = (pair_mask * left_gate * left_proj).astype(jnp.bfloat16)
    right_op = (pair_mask * right_gate * right_proj).astype(jnp.bfloat16)
    normed_out, inv_out = normalize(saved_product)
    out_gate = jax.nn.sigmoid(matmul(normed_mid, w_out_gate))
    gate_term = pair_grad * matmul(normed_out, w_out) * out_gate * (1.0 - out_gate)
    grad_normed = matmul(pair_grad * out_gate, w_out.T)
    grad_product = norm_back(normed_out, inv_out, grad_normed).astype(jnp.bfloat16)
    kept_values = (normed_in, inv_in, hidden_one, hidden_two, normed_mid, inv_mid, left_proj, left_gate, right_proj, right_gate, gate_term)
    return (grad_product, left_op, right_op, kept_values)

def local_back(pair_grad, pair_mask, kept_values, grad_left, grad_right, w_one, w_two, w_three, w_left, w_left_gate, w_right, w_right_gate, w_out_gate):
    normed_in, inv_in, hidden_one, hidden_two, normed_mid, inv_mid, left_proj, left_gate, right_proj, right_gate, gate_term = kept_values
    left_scaled = grad_left * pair_mask * left_gate
    right_scaled = grad_right * pair_mask * right_gate
    grad_mid = matmul(gate_term, w_out_gate.T)
    grad_mid = grad_mid + matmul(left_scaled, w_left.T) + matmul(left_scaled * left_proj * (1.0 - left_gate), w_left_gate.T)
    grad_mid = grad_mid + matmul(right_scaled, w_right.T) + matmul(right_scaled * right_proj * (1.0 - right_gate), w_right_gate.T)
    grad_updated = pair_grad + norm_back(normed_mid, inv_mid, grad_mid)
    grad_hidden = matmul(grad_updated, w_three.T)
    sig_one = jax.nn.sigmoid(hidden_one)
    grad_one = grad_hidden * hidden_two * sig_one * (1.0 + hidden_one * (1.0 - sig_one))
    grad_two = grad_hidden * hidden_one * sig_one
    grad_normed_in = matmul(grad_one, w_one.T) + matmul(grad_two, w_two.T)
    return grad_updated + norm_back(normed_in, inv_in, grad_normed_in)

def reference(pair_input, saved_product, pair_grad, token_mask, w_one, w_two, w_three, w_left, w_left_gate, w_right, w_right_gate, w_out, w_out_gate):
    mask_float = token_mask.astype(jnp.float32)
    pair_mask = (mask_float[:, None] * mask_float[None, :])[:, :, None]
    grad_product, left_op, right_op, kept_values = local_front(pair_input, saved_product, pair_grad, pair_mask, w_one, w_two, w_three, w_left, w_left_gate, w_right, w_right_gate, w_out, w_out_gate)
    product_wide = grad_product.astype(jnp.float32)
    grad_left = jnp.einsum('ijc,jkc->ikc', product_wide, right_op.astype(jnp.float32), precision=lax.Precision.HIGHEST)
    grad_right = jnp.einsum('ijc,ikc->jkc', product_wide, left_op.astype(jnp.float32), precision=lax.Precision.HIGHEST)
    return local_back(pair_grad, pair_mask, kept_values, grad_left, grad_right, w_one, w_two, w_three, w_left, w_left_gate, w_right, w_right_gate, w_out_gate)
```

```python
import functools

import jax
import jax.numpy as jnp
from jax import lax
from jax.experimental import pallas as pl
from jax.experimental.pallas import tpu as pltpu
from jax.sharding import PartitionSpec as P

epsilon = 1e-05
f32 = jnp.float32
bf16 = jnp.bfloat16
MESH = pl.DeviceIdType.MESH


def split(values):
    high = values.astype(bf16)
    return high, (values - high.astype(f32)).astype(bf16)


def matmul(values, high_ref, low_ref, cols=None, transposed=False):
    dims = (((1,), (1 if transposed else 0,)), ((), ()))
    high, low = split(values)
    w_high = high_ref[...] if cols is None else high_ref[:, cols[0] : cols[1]]
    w_low = low_ref[...] if cols is None else low_ref[:, cols[0] : cols[1]]
    dot = functools.partial(lax.dot_general, dimension_numbers=dims, preferred_element_type=f32)
    return dot(high, w_high) + (dot(low, w_high) + dot(high, w_low))


def sigmoid(values):
    return 0.5 * jnp.tanh(0.5 * values) + 0.5


def normalize(values):
    center = values - jnp.mean(values, axis=-1, keepdims=True)
    inv_std = lax.rsqrt(jnp.mean(center * center, axis=-1, keepdims=True) + epsilon)
    return (center * inv_std, inv_std)


def norm_back(normed, inv_std, upstream):
    mean_up = jnp.mean(upstream, axis=-1, keepdims=True)
    mean_proj = jnp.mean(upstream * normed, axis=-1, keepdims=True)
    return (upstream - mean_up - normed * mean_proj) * inv_std


def kernel(
    sizes,
    x_ref,
    s_ref,
    g_ref,
    mask_ref,
    w1_ref,
    w2_ref,
    w3_ref,
    wl_ref,
    wlg_ref,
    wr_ref,
    wrg_ref,
    wo_ref,
    wog_ref,
    out_ref,
    w12h,
    w12l,
    w3h,
    w3l,
    w5h,
    w5l,
    woh,
    wol,
    h1s,
    h2s,
    nms,
    ims,
    lgm,
    lq,
    rgm,
    rq,
    gts,
    left32,
    right32,
    gp32,
    accl,
    accr,
    gp_all,
    right_all,
    part_y,
    got_y,
    part_z,
    got_z,
    ag_send,
    ag_recv,
    fw_send,
    gp_send,
    gp_recv,
    ys_send,
    ys_recv,
    zs_send,
    zs_recv,
):
    rows, pairs, tr, tc, tokens, n_col, n_ch, chunk, ktile = sizes
    n_k = n_col * n_ch
    n_z = rows // 2
    hid = w1_ref.shape[1]
    row = lax.axis_index("row")
    my_z, my_y = row // 2, row % 2
    col, ch = lax.axis_index("col"), lax.axis_index("ch")
    my_k = col * n_ch + ch
    y_peer = my_z * 2 + (1 - my_y)
    z_steps = range(1, n_z)
    k_steps = range(1, n_k)

    def z_at(step):
        return lax.rem(my_z + step, n_z)

    def k_peer(step):
        other = lax.rem(my_k + step, n_k)
        return {"col": other // n_ch, "ch": other % n_ch}

    barrier = pltpu.get_barrier_semaphore()
    for step in z_steps:
        pl.semaphore_signal(barrier, inc=1, device_id={"row": z_at(step) * 2 + my_y}, device_id_type=MESH)
    pl.semaphore_signal(barrier, inc=1, device_id={"row": y_peer}, device_id_type=MESH)
    for step in k_steps:
        pl.semaphore_signal(barrier, inc=1, device_id=k_peer(step), device_id_type=MESH)

    def put(high_ref, low_ref, at, source):
        high, low = split(source[...])
        high_ref[:, at : at + high.shape[1]] = high
        low_ref[:, at : at + high.shape[1]] = low

    put(w12h, w12l, 0, w1_ref)
    put(w12h, w12l, hid, w2_ref)
    put(w3h, w3l, 0, w3_ref)
    for place, source in enumerate((wl_ref, wlg_ref, wr_ref, wrg_ref, wog_ref)):
        put(w5h, w5l, place * 128, source)
    put(woh, wol, 0, wo_ref)

    token = lax.broadcasted_iota(jnp.int32, (tc, tokens), 1)
    spot = lax.broadcasted_iota(jnp.int32, (tc, tokens), 0)
    mask = mask_ref[...].astype(f32)
    col_mask = jnp.sum(
        jnp.where(token == spot + my_k * tc, jnp.broadcast_to(mask, (tc, tokens)), 0.0), axis=1, keepdims=True
    )
    col_mask = jnp.concatenate([jnp.broadcast_to(col_mask, (tc, 128))] * (chunk // tc), axis=0)

    def front(step, carry):
        base = pl.multiple_of(step * chunk, chunk)
        here = pl.ds(base, chunk)
        token = lax.broadcasted_iota(jnp.int32, (chunk, tokens), 1)
        spot = lax.broadcasted_iota(jnp.int32, (chunk, tokens), 0) + base
        ahead = spot - (token - row * tr) * tc
        row_mask = jnp.sum(
            jnp.where((ahead >= 0) & (ahead < tc), jnp.broadcast_to(mask, (chunk, tokens)), 0.0), axis=1, keepdims=True
        )
        pair_mask = col_mask * row_mask
        pair_input = x_ref[here, :]
        normed_in, _ = normalize(pair_input)
        hidden = matmul(normed_in, w12h, w12l)
        hidden_one, hidden_two = hidden[:, :hid], hidden[:, hid:]
        h1s[here, :] = hidden_one
        h2s[here, :] = hidden_two
        act = hidden_one * sigmoid(hidden_one) * hidden_two
        updated = pair_input + matmul(act, w3h, w3l)
        normed_mid, inv_mid = normalize(updated)
        nms[here, :] = normed_mid
        ims[here, :] = jnp.broadcast_to(inv_mid, (chunk, 128))
        proj = matmul(normed_mid, w5h, w5l)
        right_proj, right_gate = proj[:, 256:384], sigmoid(proj[:, 384:512])
        masked = pair_mask * right_gate
        rgm[here, :] = masked
        rq[here, :] = right_proj * (1.0 - right_gate)
        right_op = (masked * right_proj).astype(bf16)
        right_all[row, here, :] = right_op
        left_proj, left_gate = proj[:, :128], sigmoid(proj[:, 128:256])
        masked = pair_mask * left_gate
        lgm[here, :] = masked
        lq[here, :] = left_proj * (1.0 - left_gate)
        left32[here, :] = (masked * left_proj).astype(bf16).astype(f32)
        out_gate = sigmoid(proj[:, 512:640])
        pair_grad = g_ref[here, :]
        normed_out, inv_out = normalize(s_ref[here, :])
        gts[here, :] = pair_grad * matmul(normed_out, woh, wol) * out_gate * (1.0 - out_gate)
        grad_normed = matmul(pair_grad * out_gate, woh, wol, transposed=True)
        gp_all[my_k, here, :] = norm_back(normed_out, inv_out, grad_normed).astype(bf16)
        return carry

    lax.fori_loop(0, pairs // chunk, front, 0)
    pl.semaphore_wait(barrier, n_z + n_k - 1)

    def right_copy(slot, sem, target):
        return pltpu.make_async_remote_copy(
            src_ref=right_all.at[slot],
            dst_ref=right_all.at[slot],
            send_sem=sem,
            recv_sem=ag_recv.at[slot],
            device_id={"row": target},
            device_id_type=MESH,
        )

    sends = []

    def start(copy):
        copy.start()
        sends.append(copy)

    for step in k_steps:
        start(
            pltpu.make_async_remote_copy(
                src_ref=gp_all.at[my_k],
                dst_ref=gp_all.at[my_k],
                send_sem=gp_send.at[step],
                recv_sem=gp_recv.at[my_k],
                device_id=k_peer(step),
                device_id_type=MESH,
            )
        )
    for step in z_steps:
        start(right_copy(row, ag_send.at[step], z_at(step) * 2 + my_y))
    start(right_copy(row, ag_send.at[0], y_peer))

    def widen(slot):
        gp32[slot] = gp_all[slot].astype(f32)

    widen(my_k)
    for step in k_steps:
        other = lax.rem(my_k + step, n_k)
        pltpu.make_async_remote_copy(
            src_ref=gp_all.at[other],
            dst_ref=gp_all.at[other],
            send_sem=gp_send.at[step],
            recv_sem=gp_recv.at[other],
            device_id=k_peer(step),
            device_id_type=MESH,
        ).wait_recv()
        widen(other)

    def block_rows(owner):
        return (owner * tr) // tc, (owner * tr) % tc

    def partial_right(owner, k_base):
        slot, offset = block_rows(owner)

        def body(i, acc):
            tile = left32[pl.ds(pl.multiple_of(i * tc + k_base, 8), ktile), :]
            return tuple(
                acc[j] + gp32[slot, pl.ds(i * tc + offset + j, 1), :] * tile for j in range(tr)
            )

        return lax.fori_loop(0, tr, body, (jnp.zeros((ktile, 128), f32),) * tr)

    k_bases = range(0, tc, ktile)

    for step in list(z_steps) + [0]:
        z_to = z_at(step)
        for k_base in k_bases:
            acc = partial_right(z_to * 2 + (1 - my_y), k_base)
            for j in range(tr):
                part_y[z_to, pl.ds(j * tc + k_base, ktile), :] = acc[j].astype(bf16)
        start(
            pltpu.make_async_remote_copy(
                src_ref=part_y.at[z_to],
                dst_ref=got_y.at[z_to],
                send_sem=ys_send.at[z_to],
                recv_sem=ys_recv.at[z_to],
                device_id={"row": y_peer},
                device_id_type=MESH,
            )
        )

    for step in z_steps:
        source = lax.rem(my_z + n_z - step, n_z) * 2 + my_y
        right_copy(source, fw_send.at[step], y_peer).wait_recv()
        start(right_copy(source, fw_send.at[step], y_peer))

    def wait_y(z_to):
        pltpu.make_async_remote_copy(
            src_ref=part_y.at[z_to],
            dst_ref=got_y.at[z_to],
            send_sem=ys_send.at[z_to],
            recv_sem=ys_recv.at[z_to],
            device_id={"row": y_peer},
            device_id_type=MESH,
        ).wait_recv()

    def z_copy(source_z, target_z, step):
        return pltpu.make_async_remote_copy(
            src_ref=part_z.at[target_z],
            dst_ref=got_z.at[source_z],
            send_sem=zs_send.at[step],
            recv_sem=zs_recv.at[source_z],
            device_id={"row": target_z * 2 + my_y},
            device_id_type=MESH,
        )

    for step in z_steps:
        z_to = z_at(step)
        for place, k_base in enumerate(k_bases):
            acc = partial_right(z_to * 2 + my_y, k_base)
            if place == 0:
                wait_y(z_to)
            for j in range(tr):
                here = pl.ds(j * tc + k_base, ktile)
                part_z[z_to, here, :] = (acc[j] + got_y[z_to, here, :].astype(f32)).astype(bf16)
        start(z_copy(my_z, z_to, step))

    for k_base in k_bases:
        acc = partial_right(row, k_base)
        for j in range(tr):
            accr[pl.ds(j * tc + k_base, ktile), :] = acc[j]
    wait_y(my_z)
    accr[...] += got_y[my_z].astype(f32)

    def middle(step, carry):
        here = pl.ds(pl.multiple_of(step * 48, 48), 48)
        hidden_one, hidden_two = h1s[here, :], h2s[here, :]
        sig_one = sigmoid(hidden_one)
        h1s[here, :] = hidden_two * sig_one * (1.0 + hidden_one * (1.0 - sig_one))
        h2s[here, :] = hidden_one * sig_one
        return carry

    lax.fori_loop(0, pairs // 48, middle, 0)

    def fold_left(owner, first):
        slot, offset = block_rows(owner)
        right32[...] = right_all[owner].astype(f32)
        for k_base in k_bases:

            def body(j, acc):
                tile = right32[pl.ds(pl.multiple_of(j * tc + k_base, 8), ktile), :]
                return tuple(
                    acc[i] + gp32[slot, pl.ds(i * tc + offset + j, 1), :] * tile for i in range(tr)
                )

            begin = tuple(
                jnp.zeros((ktile, 128), f32) if first else accl[pl.ds(i * tc + k_base, ktile), :] for i in range(tr)
            )
            acc = lax.fori_loop(0, tr, body, begin)
            for i in range(tr):
                accl[pl.ds(i * tc + k_base, ktile), :] = acc[i]

    fold_left(row, True)
    for step in z_steps:
        fold_left(lax.rem(my_z + n_z - step, n_z) * 2 + my_y, False)
    for step in range(n_z):
        source = lax.rem(my_z + n_z - step, n_z) * 2 + (1 - my_y)
        right_copy(source, ag_send.at[0], y_peer).wait_recv()
        fold_left(source, False)

    for step in z_steps:
        source = lax.rem(my_z + n_z - step, n_z)
        z_copy(source, z_at(step), step).wait_recv()
        accr[...] += got_z[source].astype(f32)

    def back(step, carry):
        here = pl.ds(pl.multiple_of(step * chunk, chunk), chunk)
        left_scaled = accl[here, :] * lgm[here, :]
        right_scaled = accr[here, :] * rgm[here, :]
        wide = jnp.concatenate(
            [left_scaled, left_scaled * lq[here, :], right_scaled, right_scaled * rq[here, :], gts[here, :]], axis=1
        )
        grad_mid = matmul(wide, w5h, w5l, transposed=True)
        grad_updated = g_ref[here, :] + norm_back(nms[here, :], ims[here, :], grad_mid)
        grad_hidden = matmul(grad_updated, w3h, w3l, transposed=True)
        both = jnp.concatenate([grad_hidden * h1s[here, :], grad_hidden * h2s[here, :]], axis=1)
        grad_normed_in = matmul(both, w12h, w12l, transposed=True)
        normed_in, inv_in = normalize(x_ref[here, :])
        out_ref[here, :] = grad_updated + norm_back(normed_in, inv_in, grad_normed_in)
        return carry

    lax.fori_loop(0, pairs // chunk, back, 0)
    for copy in sends:
        copy.wait_send()


def per_device(mesh, pair_input, saved_product, pair_grad, token_mask, *weights):
    rows = mesh.shape["row"]
    n_col, n_ch = mesh.shape["col"], mesh.shape["ch"]
    tr, tc, width = pair_input.shape
    pairs = tr * tc
    tokens = token_mask.shape[0]
    hid = weights[0].shape[1]
    chunk = pairs // (pairs // (6 * 24)) if pairs % 144 == 0 else pairs
    ktile = 24 if tc % 24 == 0 else tc
    n_k, n_z = n_col * n_ch, rows // 2
    flat = [array.reshape(pairs, width) for array in (pair_input, saved_product, pair_grad)]
    vmem = pltpu.VMEM
    dma = pltpu.SemaphoreType.DMA
    tile32 = vmem((pairs, width), f32)
    sizes = (rows, pairs, tr, tc, tokens, n_col, n_ch, chunk, ktile)
    out = pl.pallas_call(
        functools.partial(kernel, sizes),
        out_shape=jax.ShapeDtypeStruct((pairs, width), f32),
        in_specs=[pl.BlockSpec(memory_space=vmem)] * 13,
        out_specs=pl.BlockSpec(memory_space=vmem),
        scratch_shapes=[
            vmem((width, 2 * hid), bf16),
            vmem((width, 2 * hid), bf16),
            vmem((hid, width), bf16),
            vmem((hid, width), bf16),
            vmem((width, 5 * width), bf16),
            vmem((width, 5 * width), bf16),
            vmem((width, width), bf16),
            vmem((width, width), bf16),
            vmem((pairs, hid), f32),
            vmem((pairs, hid), f32),
            *([tile32] * 9),
            vmem((n_k, pairs, width), f32),
            tile32,
            tile32,
            vmem((n_k, pairs, width), bf16),
            vmem((rows, pairs, width), bf16),
            *([vmem((n_z, pairs, width), bf16)] * 4),
            dma((n_z,)),
            dma((rows,)),
            dma((n_z,)),
            dma((n_k,)),
            dma((n_k,)),
            *([dma((n_z,))] * 4),
        ],
        compiler_params=pltpu.CompilerParams(
            collective_id=0, has_side_effects=True, vmem_limit_bytes=56 * 1024 * 1024
        ),
    )(*flat, token_mask.reshape(1, tokens), *weights)
    return out.reshape(tr, tc, width)


def solution(mesh):
    tile = P(("grp", "row"), ("col", "ch"), None)
    in_specs = (tile, tile, tile, P("grp")) + (P(),) * 9
    return jax.shard_map(
        functools.partial(per_device, mesh), mesh=mesh, in_specs=in_specs, out_specs=tile, check_vma=False
    )
```

```python
import functools

import jax
import jax.numpy as jnp
from jax import lax
from jax.experimental import pallas as pl
from jax.experimental.pallas import tpu as pltpu
from jax.sharding import PartitionSpec as P

epsilon = 1e-05
f32 = jnp.float32
bf16 = jnp.bfloat16
MESH = pl.DeviceIdType.MESH


def split(values):
    high = values.astype(bf16)
    return high, (values - high.astype(f32)).astype(bf16)


def matmul(values, high_ref, low_ref, cols=None, transposed=False, parts=3):
    dims = (((1,), (1 if transposed else 0,)), ((), ()))
    high, low = split(values)
    w_high = high_ref[...] if cols is None else high_ref[:, cols[0] : cols[1]]
    w_low = low_ref[...] if cols is None else low_ref[:, cols[0] : cols[1]]
    dot = functools.partial(lax.dot_general, dimension_numbers=dims, preferred_element_type=f32)
    if parts == 2:
        return dot(high, w_high) + dot(low, w_high)
    return dot(high, w_high) + (dot(low, w_high) + dot(high, w_low))


def sigmoid(values):
    return 0.5 * jnp.tanh(0.5 * values) + 0.5


def normalize(values):
    center = values - jnp.mean(values, axis=-1, keepdims=True)
    inv_std = lax.rsqrt(jnp.mean(center * center, axis=-1, keepdims=True) + epsilon)
    return (center * inv_std, inv_std)


def norm_back(normed, inv_std, upstream):
    mean_up = jnp.mean(upstream, axis=-1, keepdims=True)
    mean_proj = jnp.mean(upstream * normed, axis=-1, keepdims=True)
    return (upstream - mean_up - normed * mean_proj) * inv_std


def kernel(
    sizes,
    x_in,
    s_in,
    g_in,
    mask_in,
    w1_in,
    w2_in,
    w3_in,
    wl_in,
    wlg_in,
    wr_in,
    wrg_in,
    wo_in,
    wog_in,
    out_ref,
    w12h,
    w12l,
    w3h,
    w3l,
    w5h,
    w5l,
    woh,
    wol,
    h1s,
    h2s,
    nms,
    ims,
    lgm,
    lq,
    rgm,
    rq,
    gts,
    left32,
    masks,
    right32,
    gp32,
    accl,
    accr,
    accr_all,
    gp_all,
    right_all,
    part_y,
    got_y,
    part_z,
    got_z,
    ag_send,
    ag_recv,
    fw_send,
    gp_send,
    gp_recv,
    ys_send,
    ys_recv,
    zs_send,
    zs_recv,
    in_sem,
    x_ref,
    s_ref,
    g_ref,
    mask_ref,
    w1_ref,
    w2_ref,
    w3_ref,
    wl_ref,
    wlg_ref,
    wr_ref,
    wrg_ref,
    wo_ref,
    wog_ref,
):
    rows, pairs, tr, tc, tokens, n_col, n_ch, chunk, ktile = sizes
    n_k = n_col * n_ch
    n_z = rows // 2
    hid = w1_in.shape[1]
    row = lax.axis_index("row")
    my_z, my_y = row // 2, row % 2
    col, ch = lax.axis_index("col"), lax.axis_index("ch")
    my_k = col * n_ch + ch
    y_peer = my_z * 2 + (1 - my_y)

    places = [(dcol, dch) for dcol in range(n_col) for dch in range(n_ch)]

    def k_place(place):
        return {"col": lax.rem(col + place[0], n_col), "ch": lax.rem(ch + place[1], n_ch)}

    def k_slot(place):
        spot = k_place(place)
        return spot["col"] * n_ch + spot["ch"]

    def z_valid(delta):
        return (my_z + delta >= 0) & (my_z + delta < n_z)

    def z_row(delta):
        return (my_z + delta) * 2 + my_y

    barrier = pltpu.get_barrier_semaphore()
    for delta in [sign * far for far in range(1, n_z) for sign in (1, -1)]:

        @pl.when(z_valid(delta))
        def _():
            pl.semaphore_signal(barrier, inc=1, device_id={"row": z_row(delta)}, device_id_type=MESH)

    pl.semaphore_signal(barrier, inc=1, device_id={"row": y_peer}, device_id_type=MESH)
    for place in places[1:]:
        pl.semaphore_signal(barrier, inc=1, device_id=k_place(place), device_id_type=MESH)

    inputs = []
    for source, target in (
        (x_in, x_ref),
        (w1_in, w1_ref),
        (w2_in, w2_ref),
        (mask_in, mask_ref),
        (w3_in, w3_ref),
        (wr_in, wr_ref),
        (wrg_in, wrg_ref),
        (wog_in, wog_ref),
        (wo_in, wo_ref),
        (s_in, s_ref),
        (g_in, g_ref),
        (wl_in, wl_ref),
        (wlg_in, wlg_ref),
    ):
        copy = pltpu.make_async_copy(source, target, in_sem.at[len(inputs)])
        copy.start()
        inputs.append(copy)
    def loaded(count):
        for _ in range(count):
            inputs.pop(0).wait()

    def put(high_ref, low_ref, at, source):
        high, low = split(source[...])
        high_ref[:, at : at + high.shape[1]] = high
        low_ref[:, at : at + high.shape[1]] = low

    loaded(7)
    put(w12h, w12l, 0, w1_ref)
    put(w12h, w12l, hid, w2_ref)
    put(w3h, w3l, 0, w3_ref)
    put(w5h, w5l, 256, wr_ref)
    put(w5h, w5l, 384, wrg_ref)

    token = lax.broadcasted_iota(jnp.int32, (tc, tokens), 1)
    spot = lax.broadcasted_iota(jnp.int32, (tc, tokens), 0)
    mask = mask_ref[...].astype(f32)
    col_mask = jnp.sum(
        jnp.where(token == spot + my_k * tc, jnp.broadcast_to(mask, (tc, tokens)), 0.0), axis=1, keepdims=True
    )
    col_mask = jnp.concatenate([jnp.broadcast_to(col_mask, (tc, 128))] * (chunk // tc), axis=0)

    def front(step, carry):
        base = pl.multiple_of(step * chunk, chunk)
        here = pl.ds(base, chunk)
        token = lax.broadcasted_iota(jnp.int32, (chunk, tokens), 1)
        spot = lax.broadcasted_iota(jnp.int32, (chunk, tokens), 0) + base
        ahead = spot - (token - row * tr) * tc
        row_mask = jnp.sum(
            jnp.where((ahead >= 0) & (ahead < tc), jnp.broadcast_to(mask, (chunk, tokens)), 0.0), axis=1, keepdims=True
        )
        pair_mask = col_mask * row_mask
        pair_input = x_ref[here, :]
        normed_in, _ = normalize(pair_input)
        hidden = matmul(normed_in, w12h, w12l)
        hidden_one, hidden_two = hidden[:, :hid], hidden[:, hid:]
        h1s[here, :] = hidden_one
        h2s[here, :] = hidden_two
        act = hidden_one * sigmoid(hidden_one) * hidden_two
        updated = pair_input + matmul(act, w3h, w3l)
        normed_mid, inv_mid = normalize(updated)
        nms[here, :] = normed_mid
        ims[here, :] = jnp.broadcast_to(inv_mid, (chunk, 128))
        proj = matmul(normed_mid, w5h, w5l, cols=(256, 512))
        right_proj, right_gate = proj[:, :128], sigmoid(proj[:, 128:256])
        masks[here, :] = pair_mask
        masked = pair_mask * right_gate
        rgm[here, :] = masked
        rq[here, :] = right_proj * (1.0 - right_gate)
        right_op = (masked * right_proj).astype(bf16)
        right_all[row, here, :] = right_op
        return carry

    lax.fori_loop(0, pairs // chunk, front, 0)
    pl.semaphore_wait(barrier, n_k + n_z - 1)

    def right_copy(slot, sem, target):
        return pltpu.make_async_remote_copy(
            src_ref=right_all.at[slot],
            dst_ref=right_all.at[slot],
            send_sem=sem,
            recv_sem=ag_recv.at[slot],
            device_id={"row": target},
            device_id_type=MESH,
        )

    sends = []

    def start(copy):
        copy.start()
        sends.append(copy)

    def start_if(cond, copy):
        pl.when(cond)(copy.start)
        held.append((cond, copy))

    held = []

    def right_send(delta):
        sem = ag_send.at[2 * abs(delta) - 1 + (delta < 0)]
        start_if(z_valid(delta), right_copy(row, sem, z_row(delta)))

    def gp_copy(place, slot):
        return pltpu.make_async_remote_copy(
            src_ref=gp_all.at[slot],
            dst_ref=gp_all.at[slot],
            send_sem=gp_send.at[places.index(place)],
            recv_sem=gp_recv.at[slot],
            device_id=k_place(place),
            device_id_type=MESH,
        )

    for far in range(1, n_z):
        right_send(far)
        right_send(-far)
    start(right_copy(row, ag_send.at[0], y_peer))

    loaded(6)
    put(w5h, w5l, 512, wog_ref)
    put(woh, wol, 0, wo_ref)
    put(w5h, w5l, 0, wl_ref)
    put(w5h, w5l, 128, wlg_ref)

    def gates(step, carry):
        here = pl.ds(pl.multiple_of(step * chunk, chunk), chunk)
        out_gate = sigmoid(matmul(nms[here, :], w5h, w5l, cols=(512, 640)))
        pair_grad = g_ref[here, :]
        normed_out, inv_out = normalize(s_ref[here, :])
        grad_normed = matmul(pair_grad * out_gate, woh, wol, transposed=True)
        gp_all[my_k, here, :] = norm_back(normed_out, inv_out, grad_normed).astype(bf16)
        gts[here, :] = pair_grad * out_gate * (1.0 - out_gate)
        return carry

    lax.fori_loop(0, pairs // chunk, gates, 0)
    for place in places[::-1][:-1]:
        start(gp_copy(place, my_k))

    def lefts(step, carry):
        here = pl.ds(pl.multiple_of(step * chunk, chunk), chunk)
        proj = matmul(nms[here, :], w5h, w5l, cols=(0, 256))
        left_proj, left_gate = proj[:, :128], sigmoid(proj[:, 128:256])
        masked = masks[here, :] * left_gate
        lgm[here, :] = masked
        lq[here, :] = left_proj * (1.0 - left_gate)
        left32[here, :] = (masked * left_proj).astype(bf16).astype(f32)
        return carry

    lax.fori_loop(0, pairs // chunk, lefts, 0)

    def widen(slot):
        gp32[slot] = gp_all[slot].astype(f32)

    def arrive(place):
        slot = k_slot(place)
        gp_copy(place, slot).wait_recv()
        widen(slot)

    widen(my_k)

    def block_rows(owner):
        return (owner * tr) // tc, (owner * tr) % tc

    def partial_right(owner, k_base):
        slot, offset = block_rows(owner)

        def body(i, acc):
            tile = left32[pl.ds(pl.multiple_of(i * tc + k_base, 8), ktile), :]
            return tuple(
                acc[j] + gp32[slot, pl.ds(i * tc + offset + j, 1), :] * tile for j in range(tr)
            )

        return lax.fori_loop(0, tr, body, (jnp.zeros((ktile, 128), f32),) * tr)

    k_bases = range(0, tc, ktile)

    per_slot = n_z // n_k

    def to_y(place):
        for q in range(per_slot):
            z_to = k_slot(place) * per_slot + q
            for k_base in k_bases:
                acc = partial_right(z_to * 2 + (1 - my_y), k_base)
                for j in range(tr):
                    part_y[z_to, pl.ds(j * tc + k_base, ktile), :] = acc[j].astype(bf16)
            start(
                pltpu.make_async_remote_copy(
                    src_ref=part_y.at[z_to],
                    dst_ref=got_y.at[z_to],
                    send_sem=ys_send.at[z_to],
                    recv_sem=ys_recv.at[z_to],
                    device_id={"row": y_peer},
                    device_id_type=MESH,
                )
            )

    def wait_y(z_to):
        pltpu.make_async_remote_copy(
            src_ref=part_y.at[z_to],
            dst_ref=got_y.at[z_to],
            send_sem=ys_send.at[z_to],
            recv_sem=ys_recv.at[z_to],
            device_id={"row": y_peer},
            device_id_type=MESH,
        ).wait_recv()

    def z_copy(source_z, target_z):
        return pltpu.make_async_remote_copy(
            src_ref=part_z.at[target_z],
            dst_ref=got_z.at[source_z],
            send_sem=zs_send.at[target_z],
            recv_sem=zs_recv.at[source_z],
            device_id={"row": target_z * 2 + my_y},
            device_id_type=MESH,
        )

    def to_z(place):
        for q in range(per_slot):
            z_to = k_slot(place) * per_slot + q
            mine = z_to == my_z
            wait_y(z_to)
            for k_base in k_bases:
                acc = partial_right(z_to * 2 + my_y, k_base)
                for j in range(tr):
                    here = pl.ds(j * tc + k_base, ktile)
                    total = acc[j] + got_y[z_to, here, :].astype(f32)
                    part_z[z_to, here, :] = total.astype(bf16)
                    accr_all[z_to, here, :] = total
            start_if(jnp.logical_not(mine), z_copy(my_z, z_to))

    def forward(delta):
        @pl.when(z_valid(delta))
        def _():
            right_copy(z_row(delta), fw_send.at[0], y_peer).wait_recv()

        sem = fw_send.at[2 * abs(delta) - 2 + (delta < 0)]
        start_if(z_valid(delta), right_copy(z_row(delta), sem, y_peer))

    def middle(step, carry):
        here = pl.ds(pl.multiple_of(step * 48, 48), 48)
        hidden_one, hidden_two = h1s[here, :], h2s[here, :]
        sig_one = sigmoid(hidden_one)
        h1s[here, :] = hidden_two * sig_one * (1.0 + hidden_one * (1.0 - sig_one))
        h2s[here, :] = hidden_one * sig_one
        return carry

    def gate_back(step, carry):
        here = pl.ds(pl.multiple_of(step * chunk, chunk), chunk)
        normed_out, _ = normalize(s_ref[here, :])
        gate_term = gts[here, :] * matmul(normed_out, woh, wol)
        gts[here, :] = matmul(gate_term, w5h, w5l, cols=(512, 640), transposed=True)
        return carry

    def left_back(step, carry):
        here = pl.ds(pl.multiple_of(step * chunk, chunk), chunk)
        scaled = accl[here, :] * lgm[here, :]
        wide = jnp.concatenate([scaled, scaled * lq[here, :]], axis=1)
        gts[here, :] += matmul(wide, w5h, w5l, cols=(0, 256), transposed=True)
        return carry

    def fold_left(owner, first):
        slot, offset = block_rows(owner)
        right32[...] = right_all[owner].astype(f32)
        for k_base in k_bases:

            def body(j, acc):
                tile = right32[pl.ds(pl.multiple_of(j * tc + k_base, 8), ktile), :]
                return tuple(
                    acc[i] + gp32[slot, pl.ds(i * tc + offset + j, 1), :] * tile for i in range(tr)
                )

            begin = tuple(
                jnp.zeros((ktile, 128), f32) if first else accl[pl.ds(i * tc + k_base, ktile), :] for i in range(tr)
            )
            acc = lax.fori_loop(0, tr, body, begin)
            for i in range(tr):
                accl[pl.ds(i * tc + k_base, ktile), :] = acc[i]

    to_y(places[0])
    arrive(places[1])
    to_y(places[1])
    lax.fori_loop(0, pairs // 48, middle, 0)
    lax.fori_loop(0, pairs // chunk, gate_back, 0)
    forward(1)
    forward(-1)
    to_z(places[0])
    for place in places[2:]:
        arrive(place)
        to_y(place)
    to_z(places[1])
    for far in range(2, n_z):
        forward(far)
        forward(-far)
        if far < len(places):
            to_z(places[far])
    for far in range(n_z, len(places)):
        to_z(places[far])

    def fold_if(delta):
        pl.when(z_valid(delta))(lambda: fold_left(z_row(delta), False))

    def fold_other(delta):
        @pl.when(z_valid(delta))
        def _():
            source = (my_z + delta) * 2 + (1 - my_y)
            right_copy(source, ag_send.at[0], y_peer).wait_recv()
            fold_left(source, False)

    deltas = [sign * far for far in range(1, n_z) for sign in (1, -1)]
    fold_left(row, True)
    fold_other(0)
    for delta in deltas:
        fold_if(delta)
    for delta in deltas:
        fold_other(delta)

    lax.fori_loop(0, pairs // chunk, left_back, 0)
    accr[...] = accr_all[my_z]
    for delta in deltas:

        @pl.when(z_valid(delta))
        def _():
            z_copy(my_z + delta, my_z + delta).wait_recv()
            accr[...] += got_z[my_z + delta].astype(f32)

    def back(step, carry):
        here = pl.ds(pl.multiple_of(step * chunk, chunk), chunk)
        right_scaled = accr[here, :] * rgm[here, :]
        wide = jnp.concatenate([right_scaled, right_scaled * rq[here, :]], axis=1)
        grad_mid = gts[here, :] + matmul(wide, w5h, w5l, cols=(256, 512), transposed=True)
        grad_updated = g_ref[here, :] + norm_back(nms[here, :], ims[here, :], grad_mid)
        grad_hidden = matmul(grad_updated, w3h, w3l, transposed=True, parts=2)
        both = jnp.concatenate([grad_hidden * h1s[here, :], grad_hidden * h2s[here, :]], axis=1)
        grad_normed_in = matmul(both, w12h, w12l, transposed=True, parts=2)
        normed_in, inv_in = normalize(x_ref[here, :])
        out_ref[here, :] = grad_updated + norm_back(normed_in, inv_in, grad_normed_in)
        return carry

    lax.fori_loop(0, pairs // chunk, back, 0)
    for copy in sends:
        copy.wait_send()
    for cond, copy in held:
        pl.when(cond)(copy.wait_send)


def per_device(mesh, pair_input, saved_product, pair_grad, token_mask, *weights):
    rows = mesh.shape["row"]
    n_col, n_ch = mesh.shape["col"], mesh.shape["ch"]
    tr, tc, width = pair_input.shape
    pairs = tr * tc
    tokens = token_mask.shape[0]
    hid = weights[0].shape[1]
    chunk = pairs // (pairs // (6 * 24)) if pairs % 144 == 0 else pairs
    ktile = 24 if tc % 24 == 0 else tc
    n_k, n_z = n_col * n_ch, rows // 2
    flat = [array.reshape(pairs, width) for array in (pair_input, saved_product, pair_grad)]
    arrays = [*flat, token_mask.reshape(1, tokens), *weights]
    vmem = pltpu.VMEM
    dma = pltpu.SemaphoreType.DMA
    tile32 = vmem((pairs, width), f32)
    sizes = (rows, pairs, tr, tc, tokens, n_col, n_ch, chunk, ktile)
    out = pl.pallas_call(
        functools.partial(kernel, sizes),
        out_shape=jax.ShapeDtypeStruct((pairs, width), f32),
        in_specs=[pl.BlockSpec(memory_space=pl.ANY)] * 13,
        out_specs=pl.BlockSpec(memory_space=vmem),
        scratch_shapes=[
            vmem((width, 2 * hid), bf16),
            vmem((width, 2 * hid), bf16),
            vmem((hid, width), bf16),
            vmem((hid, width), bf16),
            vmem((width, 5 * width), bf16),
            vmem((width, 5 * width), bf16),
            vmem((width, width), bf16),
            vmem((width, width), bf16),
            vmem((pairs, hid), f32),
            vmem((pairs, hid), f32),
            *([tile32] * 10),
            vmem((n_k, pairs, width), f32),
            tile32,
            tile32,
            vmem((n_z, pairs, width), f32),
            vmem((n_k, pairs, width), bf16),
            vmem((rows, pairs, width), bf16),
            *([vmem((n_z, pairs, width), bf16)] * 4),
            dma((2 * n_z,)),
            dma((rows,)),
            dma((2 * n_z,)),
            dma((n_k,)),
            dma((n_k,)),
            *([dma((n_z,))] * 4),
            dma((13,)),
            *[vmem(array.shape, array.dtype) for array in arrays],
        ],
        compiler_params=pltpu.CompilerParams(
            collective_id=0, has_side_effects=True, vmem_limit_bytes=56 * 1024 * 1024
        ),
    )(*arrays)
    return out.reshape(tr, tc, width)


def solution(mesh):
    tile = P(("grp", "row"), ("col", "ch"), None)
    in_specs = (tile, tile, tile, P("grp")) + (P(),) * 9
    return jax.shard_map(
        functools.partial(per_device, mesh), mesh=mesh, in_specs=in_specs, out_specs=tile, check_vma=False
    )
```
